32 devices in a mesh: region: 2 (over x), var: 8 (over z, y), samp: 2 (over core).
Axes of the slice: x: 2, y: 2, z: 4, core: 2. Of those that a mesh axis runs over, the one named last changes fastest.
Arguments:
- dosage: bfloat16 [2048, 16384], P('samp', ('region', 'var')), parts along dimension 1, may hold values from 0 to 2
- observed: int32 [2048, 16384], P('samp', ('region', 'var')), parts along dimension 1, may hold values from 0 to 1, as said below
- counts: int32 [16], P(('region', 'var')), parts along dimension 0, may hold values from 1 to 4, as said below
Outputs:
- correlations: bfloat16 [16, 4, 1024, 1024], P(('region', 'var'), None, 'samp'), parts along dimension 0
The draws below stay inside these ranges and needn't reach their ends.
There are 2 independent parts, one for each index of `region`. The reference program is written for one: setup_inputs(seed, part) draws one part's arguments, and reference() takes and returns one part's arrays. A program takes and returns all parts, laid end to end along the dimension named above; each array names one. Nothing has to cross between parts.
Inputs may be any that keep to these rules, and one draw needn't show every extreme that they name: Block b's partners are blocks b to b + counts[b] - 1; counts[b] is at most 8 - b, and counts[0] = 4. `observed`: some variants are missing in every sample.
All inputs are finite; a program needn't handle non-finite values.
Results may differ from the reference program's by a relative error of at most 0.001.
The reference program's roundings to bfloat16 on the way (of `scored`) count: a program that leaves them out, or rounds other values in their place, can miss the bound.
Values may be sent and summed in bfloat16 or wider, within the bound.
A program may use at most 128 MiB of HBM per device.

```python
import jax
import jax.numpy as jnp
from jax import lax

BLK = 1024
WIN = 4
NBLK = 8
V = 8192
S = 2048


def draw_dosage(key, part):
    spacings = [16, 128, 1024, 4096]
    strengths = [0.25, 0.25, 0.35, 0.45]
    column = jnp.arange(V, dtype=jnp.int32)
    smooth = jnp.zeros((S, V), jnp.float32)
    for number in range(4):
        spacing = spacings[number]
        anchors = jax.random.normal(jax.random.fold_in(key, 11 + number), (S, V // spacing + 2), jnp.float32)
        index = column // spacing
        weight = (column % spacing).astype(jnp.float32) / spacing
        smooth = smooth + strengths[number] * (anchors[:, index] * (1.0 - weight) + anchors[:, index + 1] * weight)
    base = jax.random.uniform(jax.random.fold_in(key, 21), (1, V), jnp.float32, 0.3, 1.7)
    noise = 0.25 * jax.random.normal(jax.random.fold_in(key, 22), (S, V), jnp.float32)
    return jnp.clip(base + smooth + noise, 0.0, 2.0).astype(jnp.bfloat16)


def draw_observed(key, part):
    entries = jax.random.randint(jax.random.fold_in(key, 41), (S, V), 0, 10, dtype=jnp.int32)
    present = (entries < 9).astype(jnp.int32)
    lottery = jax.random.randint(jax.random.fold_in(key, 42), (V,), 0, 64, dtype=jnp.int32)
    forced = jax.random.randint(jax.random.fold_in(key, 43), (), 0, V, dtype=jnp.int32)
    column = jnp.arange(V, dtype=jnp.int32)
    missing = jnp.logical_or(lottery == 0, column == forced)
    return jnp.where(missing[None, :], jnp.zeros_like(present), present)


def draw_counts(key, part):
    drawn = jax.random.randint(jax.random.fold_in(key, 31), (NBLK,), 1, WIN + 1, dtype=jnp.int32)
    limit = NBLK - jnp.arange(NBLK, dtype=jnp.int32)
    capped = jnp.minimum(drawn, limit)
    return capped.at[0].set(WIN)


def setup_inputs(seed: int = 0, part: int = 0) -> dict:
    key_list = jax.random.split(jax.random.key(seed), 4)
    own_keys = jax.random.split(jax.random.fold_in(key_list[3], part), 4)
    return {
        "dosage": draw_dosage(jax.random.fold_in(jax.random.fold_in(key_list[3], part), 71), part),
        "observed": draw_observed(jax.random.fold_in(jax.random.fold_in(key_list[3], part), 71), part),
        "counts": draw_counts(jax.random.fold_in(jax.random.fold_in(key_list[3], part), 71), part),
    }


def reference(dosage, observed, counts):
    values = dosage.astype(jnp.float32)
    present = observed.astype(jnp.float32)
    present_count = jnp.maximum(lax.optimization_barrier(jnp.sum(present, axis=0)), 1.0)
    center = lax.optimization_barrier(jnp.sum(present * values, axis=0)) / present_count
    offsets = present * (values - center)
    spread = lax.optimization_barrier(jnp.sum(offsets * offsets, axis=0)) / present_count
    scored = (offsets * lax.rsqrt(spread + 1e-05)).astype(jnp.bfloat16)

    def one_block(block):
        own = lax.dynamic_slice_in_dim(scored, block * BLK, BLK, 1)
        tiles = []
        for offset in range(WIN):
            target = jnp.minimum(block + offset, NBLK - 1).astype(jnp.int32)
            partner = lax.dynamic_slice_in_dim(scored, target * BLK, BLK, 1)
            product = jnp.dot(own.T, partner, preferred_element_type=jnp.float32) / S
            keep = offset < counts[block]
            tiles.append(jnp.where(keep, product, jnp.zeros_like(product)))
        return jnp.stack(tiles).astype(jnp.bfloat16)
    return lax.map(one_block, jnp.arange(NBLK, dtype=jnp.int32))
```

```python
import functools

import jax
import jax.numpy as jnp
from jax import lax
from jax.experimental import pallas as pl
from jax.experimental.pallas import tpu as pltpu
from jax.sharding import PartitionSpec as P

WIN = 4

epsilon = 1e-05

PIECES = 4
ROWS = 128


def kernel(
    n,
    total,
    d_ref,
    o_ref,
    out_ref,
    s0,
    s1,
    s2,
    t0,
    tm,
    r3s,
    r3r,
    stat_mine,
    stat_other,
    obuf,
    stat_sem,
    own_sem,
    down_sem,
    up_sem,
    y_sem,
    x1_sem,
    x2_sem,
    r3_sem,
    out_sem,
):
    b = lax.axis_index("var")
    c = lax.axis_index("samp")
    even = lax.rem(b, 2) == 0
    pair = b + 1 - 2 * lax.rem(b, 2)
    has_up = b + 2 < n
    has_down = b >= 2
    has_one = jnp.logical_or(even, has_up)
    core = {"samp": 1 - c}
    chunks, full, width = s0.shape
    half = chunks // 2
    local = full // 2
    steps = local // ROWS
    groups = ROWS // 8
    piece = full // PIECES
    tpiece = width // PIECES

    def remote(src, dst, sem, where):
        return pltpu.make_async_remote_copy(
            src_ref=src,
            dst_ref=dst,
            send_sem=sem.at[0],
            recv_sem=sem.at[1],
            device_id=where,
            device_id_type=pl.DeviceIdType.MESH,
        )

    barrier = pltpu.get_barrier_semaphore()
    pl.semaphore_signal(barrier, inc=1, device_id=core, device_id_type=pl.DeviceIdType.MESH)
    pl.semaphore_signal(
        barrier, inc=1, device_id={"var": pair}, device_id_type=pl.DeviceIdType.MESH
    )

    @pl.when(has_up)
    def _():
        pl.semaphore_signal(
            barrier, inc=1, device_id={"var": b + 2}, device_id_type=pl.DeviceIdType.MESH
        )

    @pl.when(has_down)
    def _():
        pl.semaphore_signal(
            barrier, inc=1, device_id={"var": b - 2}, device_id_type=pl.DeviceIdType.MESH
        )

    def column(ch):
        return pl.ds(ch * width, width)

    def load(ch, r):
        rows = pl.ds(pl.multiple_of(r * ROWS, ROWS), ROWS)
        present = o_ref[rows, column(ch)].astype(jnp.float32)
        return present, d_ref[rows, column(ch)].astype(jnp.float32)

    def fold(x):
        return jnp.sum(x.reshape(groups, 8, width), axis=0)

    stat_mine[...] = jnp.zeros_like(stat_mine)
    for ch in range(chunks):
        zero = jnp.zeros((8, width), jnp.float32)

        def first(r, carry):
            present, values = load(ch, r)
            return carry[0] + fold(present), carry[1] + fold(present * values)

        count8, sum8 = lax.fori_loop(0, steps, first, (zero, zero))
        count = jnp.sum(count8, axis=0, keepdims=True)
        summed = jnp.sum(sum8, axis=0, keepdims=True)
        mean = summed / jnp.maximum(count, 1.0)

        def second(r, carry):
            present, values = load(ch, r)
            off = present * (values - mean)
            return carry + fold(off * off)

        square = jnp.sum(lax.fori_loop(0, steps, second, zero), axis=0, keepdims=True)
        stat_mine[0:1, column(ch)] = count
        stat_mine[1:2, column(ch)] = summed
        stat_mine[2:3, column(ch)] = square

    pl.semaphore_wait(barrier, 2 + has_up.astype(jnp.int32) + has_down.astype(jnp.int32))

    stat_copy = remote(stat_mine, stat_other, stat_sem, core)
    stat_copy.start()
    stat_copy.wait()

    def own_copy(i, who):
        rows = pl.ds(pl.multiple_of(c * local, local), local)
        ref = s0.at[who * half + i, rows, :]
        return remote(ref, ref, own_sem.at[i], core)

    for order in range(2):
        who = (1 - c) if order == 0 else c
        for i in range(half):
            ch = who * half + i
            cols = pl.ds(pl.multiple_of(ch * width, width), width)
            n_a, n_b = stat_mine[0:1, cols], stat_other[0:1, cols]
            s_a, s_b = stat_mine[1:2, cols], stat_other[1:2, cols]
            count = jnp.maximum(n_a + n_b, 1.0)
            center = (s_a + s_b) / count
            gap_a = s_a / jnp.maximum(n_a, 1.0) - center
            gap_b = s_b / jnp.maximum(n_b, 1.0) - center
            square = (stat_mine[2:3, cols] + n_a * gap_a * gap_a) + (
                stat_other[2:3, cols] + n_b * gap_b * gap_b
            )
            scale = lax.rsqrt(square / count + epsilon)

            def third(r, carry):
                rows = pl.ds(pl.multiple_of(r * ROWS, ROWS), ROWS)
                present = o_ref[rows, cols].astype(jnp.float32)
                values = d_ref[rows, cols].astype(jnp.float32)
                out = (present * (values - center) * scale).astype(jnp.bfloat16)
                s0[ch, pl.ds(pl.multiple_of(c * local + r * ROWS, ROWS), ROWS), :] = out
                return carry

            lax.fori_loop(0, steps, third, 0)
            if order == 0:
                own_send(s0, remote, own_sem, ch, c, local, i, core).start()

    for i in range(half):
        ch = c * half + i
        own_recv(s0, remote, own_sem, ch, c, local, i, core).wait_recv()

        def down(p):
            ref = s0.at[ch, pl.ds(pl.multiple_of(p * piece, piece), piece), :]
            to = s2.at[ch, pl.ds(pl.multiple_of(p * piece, piece), piece), :]
            return remote(ref, to, down_sem.at[i * PIECES + p], {"var": b - 2})

        def sideways(p):
            ref = s0.at[ch, pl.ds(pl.multiple_of(p * piece, piece), piece), :]
            to = s1.at[ch, pl.ds(pl.multiple_of(p * piece, piece), piece), :]
            return remote(ref, to, y_sem.at[i * PIECES + p], {"var": pair})

        for p in range(PIECES):

            @pl.when(has_down)
            def _():
                down(p).start()

            @pl.when(jnp.logical_not(even))
            def _():
                sideways(p).start()

        for q in range(PIECES):
            t0[i * width : (i + 1) * width, q * piece : (q + 1) * piece] = s0[
                ch, q * piece : (q + 1) * piece, :
            ].T

        @pl.when(has_up)
        def _():
            for p in range(PIECES):
                rows = pl.ds(i * width + p * tpiece, tpiece)
                remote(
                    t0.at[rows, :], tm.at[rows, :], up_sem.at[i * PIECES + p], {"var": b + 2}
                ).start()

    rows_mine = pl.ds(pl.multiple_of(c * local, local), local)
    for i in range(half):
        ref = s0.at[c * half + i, rows_mine, :]
        remote(ref, ref, own_sem.at[half + i], core).start()

    def tile(k, rhs, ch):
        acc = jnp.dot(t0[...], rhs[ch], preferred_element_type=jnp.float32)
        cols = pl.ds(pl.multiple_of(ch * width, width), width)
        obuf[k, :, cols] = (acc * (1.0 / total)).astype(jnp.bfloat16)

    def own_tile(i, carry):
        tile(0, s0, c * half + i)
        return carry

    lax.fori_loop(0, half, own_tile, 0)
    for i in range(half):
        ref = s0.at[(1 - c) * half + i, pl.ds(pl.multiple_of((1 - c) * local, local), local), :]
        remote(ref, ref, own_sem.at[half + i], core).wait_recv()

    def other_tile(i, carry):
        tile(0, s0, (1 - c) * half + i)
        return carry

    lax.fori_loop(0, half, other_tile, 0)

    def store(k):
        return pltpu.make_async_copy(obuf.at[k], out_ref.at[k], out_sem.at[k])

    store(0).start()

    def part(ref, ch, p):
        return ref.at[ch, pl.ds(pl.multiple_of(p * piece, piece), piece), :]

    for i in range(half):
        mine = c * half + i
        theirs = (1 - c) * half + i

        def relay(p, carry):
            slot = i * PIECES + p

            @pl.when(has_up)
            def _():
                got = part(s2, mine, p)
                remote(got, got, down_sem.at[slot], {"var": b + 2}).wait_recv()
                remote(got, got, x2_sem.at[slot], core).start()

                @pl.when(even)
                def _():
                    remote(got, part(s1, mine, p), y_sem.at[slot], {"var": pair}).start()

            @pl.when(has_one)
            def _():
                got = part(s1, mine, p)
                remote(got, got, y_sem.at[slot], {"var": pair}).wait_recv()
                remote(got, got, x1_sem.at[slot], core).start()

            return carry

        lax.fori_loop(0, PIECES, relay, 0)

        @pl.when(has_one)
        def _():
            tile(1, s1, mine)

        @pl.when(has_up)
        def _():
            tile(2, s2, mine)

        if i == half - 1:

            @pl.when(has_down)
            def _():
                for slot in range(half * PIECES):
                    rows = pl.ds(slot * tpiece, tpiece)
                    remote(
                        tm.at[rows, :], tm.at[rows, :], up_sem.at[slot], {"var": b - 2}
                    ).wait_recv()

        def received(p, carry):
            slot = i * PIECES + p

            @pl.when(has_up)
            def _():
                got = part(s2, theirs, p)
                remote(got, got, x2_sem.at[slot], core).wait_recv()

            @pl.when(has_one)
            def _():
                got = part(s1, theirs, p)
                remote(got, got, x1_sem.at[slot], core).wait_recv()

            return carry

        lax.fori_loop(0, PIECES, received, 0)

        @pl.when(has_one)
        def _():
            tile(1, s1, theirs)

        @pl.when(has_up)
        def _():
            tile(2, s2, theirs)

    @pl.when(jnp.logical_and(has_down, has_one))
    def _():
        def behind(ch, carry):
            acc = jnp.dot(tm[...], s1[ch], preferred_element_type=jnp.float32)
            r3s[ch] = (acc * (1.0 / total)).astype(jnp.bfloat16)
            remote(r3s.at[ch], r3r.at[ch], r3_sem.at[ch], {"var": b - 2}).start()
            return carry

        lax.fori_loop(0, chunks, behind, 0)

    store(1).start()
    store(2).start()

    @pl.when(jnp.logical_and(has_up, jnp.logical_or(even, b + 4 < n)))
    def _():
        def arrive(ch, carry):
            remote(r3r.at[ch], r3r.at[ch], r3_sem.at[ch], {"var": b + 2}).wait_recv()
            obuf[3, :, pl.ds(pl.multiple_of(ch * width, width), width)] = r3r[ch]
            return carry

        lax.fori_loop(0, chunks, arrive, 0)

    store(3).start()

    for i in range(half):
        own_send(s0, remote, own_sem, (1 - c) * half + i, c, local, i, core).wait_send()
        ref = s0.at[c * half + i, rows_mine, :]
        remote(ref, ref, own_sem.at[half + i], core).wait_send()

    def drain(slot, carry):
        i = slot // PIECES
        p = lax.rem(slot, PIECES)
        ch = c * half + i
        rows = pl.ds(pl.multiple_of(slot * tpiece, tpiece), tpiece)

        @pl.when(has_down)
        def _():
            ref = part(s0, ch, p)
            remote(ref, ref, down_sem.at[slot], {"var": b - 2}).wait_send()

        @pl.when(jnp.logical_or(jnp.logical_not(even), has_up))
        def _():
            ref = part(s0, ch, p)
            remote(ref, ref, y_sem.at[slot], {"var": pair}).wait_send()

        @pl.when(has_up)
        def _():
            remote(t0.at[rows, :], t0.at[rows, :], up_sem.at[slot], {"var": b + 2}).wait_send()
            ref = part(s2, ch, p)
            remote(ref, ref, x2_sem.at[slot], core).wait_send()

        @pl.when(has_one)
        def _():
            ref = part(s1, ch, p)
            remote(ref, ref, x1_sem.at[slot], core).wait_send()

        return carry

    lax.fori_loop(0, half * PIECES, drain, 0)

    @pl.when(jnp.logical_and(has_down, has_one))
    def _():
        def sent(ch, carry):
            remote(r3s.at[ch], r3s.at[ch], r3_sem.at[ch], {"var": b - 2}).wait_send()
            return carry

        lax.fori_loop(0, chunks, sent, 0)

    for k in range(WIN):
        store(k).wait()


def own_send(s0, remote, own_sem, ch, c, local, i, core):
    ref = s0.at[ch, pl.ds(pl.multiple_of(c * local, local), local), :]
    return remote(ref, ref, own_sem.at[i], core)


def own_recv(s0, remote, own_sem, ch, c, local, i, core):
    ref = s0.at[ch, pl.ds(pl.multiple_of((1 - c) * local, local), local), :]
    return remote(ref, ref, own_sem.at[i], core)


def per_device(dosage, observed, counts):
    local, variants = dosage.shape
    n = lax.axis_size("var")
    full = local * lax.axis_size("samp")
    half = variants // 2
    width = 256
    chunks = variants // width
    slots = (chunks // 2) * PIECES
    dma = pltpu.SemaphoreType.DMA
    tiles = pl.pallas_call(
        functools.partial(kernel, n, float(full)),
        out_shape=jax.ShapeDtypeStruct((WIN, half, variants), jnp.bfloat16),
        in_specs=[pl.BlockSpec(memory_space=pltpu.VMEM)] * 2,
        out_specs=pl.BlockSpec(memory_space=pl.ANY),
        scratch_shapes=[
            pltpu.VMEM((chunks, full, width), jnp.bfloat16),
            pltpu.VMEM((chunks, full, width), jnp.bfloat16),
            pltpu.VMEM((chunks, full, width), jnp.bfloat16),
            pltpu.VMEM((half, full), jnp.bfloat16),
            pltpu.VMEM((half, full), jnp.bfloat16),
            pltpu.VMEM((chunks, half, width), jnp.bfloat16),
            pltpu.VMEM((chunks, half, width), jnp.bfloat16),
            pltpu.VMEM((8, variants), jnp.float32),
            pltpu.VMEM((8, variants), jnp.float32),
            pltpu.VMEM((WIN, half, variants), jnp.bfloat16),
            dma((2,)),
            dma((chunks, 2)),
            dma((slots, 2)),
            dma((slots, 2)),
            dma((slots, 2)),
            dma((slots, 2)),
            dma((slots, 2)),
            dma((chunks, 2)),
            dma((WIN,)),
        ],
        compiler_params=pltpu.CompilerParams(
            collective_id=0, has_side_effects=True, vmem_limit_bytes=50 * 1024 * 1024
        ),
    )(dosage, observed)
    keep = jnp.arange(WIN, dtype=jnp.int32)[:, None, None] < counts[0]
    return jnp.where(keep, tiles, jnp.zeros_like(tiles))[None]


def solution(mesh):
    in_specs = (P("samp", ("region", "var")), P("samp", ("region", "var")), P(("region", "var")))
    out_specs = P(("region", "var"), None, "samp", None)
    return jax.shard_map(
        per_device, mesh=mesh, in_specs=in_specs, out_specs=out_specs, check_vma=False
    )
```

```python
import functools

import jax
import jax.numpy as jnp
from jax import lax
from jax.experimental import pallas as pl
from jax.experimental.pallas import tpu as pltpu
from jax.sharding import PartitionSpec as P

WIN = 4

epsilon = 1e-05

PIECES = 4
ROWS = 128
INPUT = pltpu.HBM
VMEM_LIMIT = 38 * 1024 * 1024


def kernel(
    n,
    total,
    d_hbm,
    o_hbm,
    out_ref,
    d_ref,
    o_ref,
    s0,
    s1,
    s2,
    t0,
    tm,
    r3s,
    r3r,
    stat_mine,
    stat_other,
    obuf,
    in_sem,
    stat_sem,
    own_sem,
    down_sem,
    up_sem,
    y_sem,
    x1_sem,
    x2_sem,
    r3_sem,
    out_sem,
    out3_sem,
):
    b = lax.axis_index("var")
    c = lax.axis_index("samp")
    even = lax.rem(b, 2) == 0
    odd = jnp.logical_not(even)
    pair = b + 1 - 2 * lax.rem(b, 2)
    has_up = b + 2 < n
    has_down = b >= 2
    has_one = jnp.logical_or(even, has_up)
    sends_back = jnp.logical_and(has_down, has_one)
    gets_back = jnp.logical_and(has_up, jnp.logical_or(even, b + 4 < n))
    core = {"samp": 1 - c}
    below, above, beside = {"var": b - 2}, {"var": b + 2}, {"var": pair}
    chunks, full, width = s0.shape
    half = chunks // 2
    local = full // 2
    steps = local // ROWS
    groups = ROWS // 8
    piece = full // PIECES
    tpiece = width // PIECES
    mesh_id = pl.DeviceIdType.MESH

    def load(ch):
        cols = pl.ds(pl.multiple_of(ch * width, width), width)
        return (
            pltpu.make_async_copy(o_hbm.at[:, cols], o_ref.at[ch], in_sem.at[ch, 0]),
            pltpu.make_async_copy(d_hbm.at[:, cols], d_ref.at[ch], in_sem.at[ch, 1]),
        )

    for i in range(half):
        for who in range(2):
            for copy in load(who * half + i):
                copy.start()

    def remote(src, dst, sem, where):
        return pltpu.make_async_remote_copy(
            src_ref=src,
            dst_ref=dst,
            send_sem=sem.at[0],
            recv_sem=sem.at[1],
            device_id=where,
            device_id_type=mesh_id,
        )

    barrier = pltpu.get_barrier_semaphore()
    pl.semaphore_signal(barrier, inc=1, device_id=core, device_id_type=mesh_id)
    pl.semaphore_signal(barrier, inc=1, device_id=beside, device_id_type=mesh_id)

    @pl.when(has_up)
    def _():
        pl.semaphore_signal(barrier, inc=1, device_id=above, device_id_type=mesh_id)

    @pl.when(has_down)
    def _():
        pl.semaphore_signal(barrier, inc=1, device_id=below, device_id_type=mesh_id)

    def fold(x):
        return jnp.sum(x.reshape(groups, 8, width), axis=0)

    def block_rows(r):
        return pl.ds(pl.multiple_of(r * ROWS, ROWS), ROWS)

    def read(ch, r):
        present = o_ref[ch, block_rows(r), :].astype(jnp.float32)
        return present, d_ref[ch, block_rows(r), :].astype(jnp.float32)

    stat_mine[...] = jnp.zeros_like(stat_mine)

    def sums(i):
        for who in range(2):
            ch = who * half + i
            for copy in load(ch):
                copy.wait()
            zero = jnp.zeros((8, width), jnp.float32)

            def first(r, carry):
                present, values = read(ch, r)
                return carry[0] + fold(present), carry[1] + fold(present * values)

            count8, sum8 = lax.fori_loop(0, steps, first, (zero, zero))
            count = jnp.sum(count8, axis=0, keepdims=True)
            summed = jnp.sum(sum8, axis=0, keepdims=True)
            mean = summed / jnp.maximum(count, 1.0)

            def second(r, carry):
                present, values = read(ch, r)
                off = present * (values - mean)
                return carry + fold(off * off)

            square = jnp.sum(lax.fori_loop(0, steps, second, zero), axis=0, keepdims=True)
            cols = slice(who * width, (who + 1) * width)
            stat_mine[i, 0:1, cols] = count
            stat_mine[i, 1:2, cols] = summed
            stat_mine[i, 2:3, cols] = square

    def stat_copy(i):
        return remote(stat_mine.at[i], stat_other.at[i], stat_sem.at[i], core)

    sums(0)
    pl.semaphore_wait(barrier, 2 + has_up.astype(jnp.int32) + has_down.astype(jnp.int32))
    stat_copy(0).start()

    def samples_of(who, ch):
        return s0.at[ch, pl.ds(pl.multiple_of(who * local, local), local), :]

    def score(who, i):
        ch = who * half + i
        cols = pl.ds(pl.multiple_of(who * width, width), width)
        n_a, n_b = stat_mine[i, 0:1, cols], stat_other[i, 0:1, cols]
        s_a, s_b = stat_mine[i, 1:2, cols], stat_other[i, 1:2, cols]
        count = jnp.maximum(n_a + n_b, 1.0)
        center = (s_a + s_b) / count
        gap_a = s_a / jnp.maximum(n_a, 1.0) - center
        gap_b = s_b / jnp.maximum(n_b, 1.0) - center
        square = (stat_mine[i, 2:3, cols] + n_a * gap_a * gap_a) + (
            stat_other[i, 2:3, cols] + n_b * gap_b * gap_b
        )
        scale = lax.rsqrt(square / count + epsilon)

        def third(r, carry):
            present, values = read(ch, r)
            out = (present * (values - center) * scale).astype(jnp.bfloat16)
            s0[ch, pl.ds(pl.multiple_of(c * local + r * ROWS, ROWS), ROWS), :] = out
            return carry

        lax.fori_loop(0, steps, third, 0)

    def part(ref, ch, p):
        at = lax.rem(p + c * (PIECES // 2), PIECES)
        return ref.at[ch, pl.ds(pl.multiple_of(at * piece, piece), piece), :]

    def send_pieces(i, pieces):
        ch = c * half + i
        for p in pieces:
            slot = i * PIECES + p

            @pl.when(has_down)
            def _():
                remote(part(s0, ch, p), part(s2, ch, p), down_sem.at[slot], below).start()

            @pl.when(odd)
            def _():
                remote(part(s0, ch, p), part(s1, ch, p), y_sem.at[slot], beside).start()

    def own_out(i):
        ref = samples_of(c, (1 - c) * half + i)
        return remote(ref, ref, own_sem.at[i], core)

    def own_in(i):
        ref = samples_of(1 - c, c * half + i)
        return remote(ref, ref, own_sem.at[i], core)

    def second_out(i):
        ref = samples_of(c, c * half + i)
        return remote(ref, ref, own_sem.at[half + i], core)

    def second_in(i):
        ref = samples_of(1 - c, (1 - c) * half + i)
        return remote(ref, ref, own_sem.at[half + i], core)

    for i in range(half):
        later = i + 1 if i + 1 < half else None
        stat_copy(i).wait()
        score(c, i)
        if i == 0:
            send_pieces(i, range(PIECES // 2))
        score(1 - c, i)
        own_out(i).start()
        if later is not None:
            sums(later)
            stat_copy(later).start()
        own_in(i).wait_recv()
        if i == 0:
            send_pieces(i, range(PIECES // 2, PIECES))
        else:
            send_pieces(i, range(PIECES))
        ch = c * half + i
        for q in range(PIECES):
            t0[i * width : (i + 1) * width, q * piece : (q + 1) * piece] = s0[
                ch, q * piece : (q + 1) * piece, :
            ].T

        @pl.when(has_up)
        def _():
            for p in range(PIECES):
                rows = pl.ds(i * width + p * tpiece, tpiece)
                slot = i * PIECES + p
                remote(t0.at[rows, :], tm.at[rows, :], up_sem.at[slot], above).start()

    for i in range(half):
        second_out(i).start()

    def tile(k, rhs, ch):
        acc = jnp.dot(t0[...], rhs[ch], preferred_element_type=jnp.float32)
        cols = pl.ds(pl.multiple_of(ch * width, width), width)
        obuf[k, :, cols] = (acc * (1.0 / total)).astype(jnp.bfloat16)

    def own_tile(i, carry):
        tile(0, s0, c * half + i)
        return carry

    lax.fori_loop(0, half, own_tile, 0)
    for i in range(half):
        second_in(i).wait_recv()

    def other_tile(i, carry):
        tile(0, s0, (1 - c) * half + i)
        return carry

    lax.fori_loop(0, half, other_tile, 0)

    def store(k):
        return pltpu.make_async_copy(obuf.at[k], out_ref.at[k], out_sem.at[k])

    store(0).start()

    def relay_two(i, p):
        slot = i * PIECES + p

        @pl.when(has_up)
        def _():
            got = part(s2, c * half + i, p)
            remote(got, got, down_sem.at[slot], above).wait_recv()

            @pl.when(even)
            def _():
                remote(got, part(s1, c * half + i, p), y_sem.at[slot], beside).start()

            remote(got, got, x2_sem.at[slot], core).start()

    def relay_one(i, p):
        slot = i * PIECES + p

        @pl.when(has_one)
        def _():
            got = part(s1, c * half + i, p)
            remote(got, got, y_sem.at[slot], beside).wait_recv()
            remote(got, got, x1_sem.at[slot], core).start()

    def received(ref, sem, i):
        def one(p, carry):
            got = part(ref, (1 - c) * half + i, p)
            remote(got, got, sem.at[i * PIECES + p], core).wait_recv()
            return carry

        lax.fori_loop(0, PIECES, one, 0)

    def turned(i):
        @pl.when(has_down)
        def _():
            for p in range(PIECES):
                rows = pl.ds(i * width + p * tpiece, tpiece)
                ref = tm.at[rows, :]
                remote(ref, ref, up_sem.at[i * PIECES + p], below).wait_recv()

    def back_copy(h, ch, where):
        return remote(r3s.at[h, ch], r3r.at[h, ch], r3_sem.at[h, ch], where)

    def behind(h, ch):
        acc = jnp.dot(
            tm[h * width : (h + 1) * width, :], s1[ch], preferred_element_type=jnp.float32
        )
        r3s[h, ch] = (acc * (1.0 / total)).astype(jnp.bfloat16)
        back_copy(h, ch, below).start()

    for i in range(half):
        mine = c * half + i
        theirs = (1 - c) * half + i
        last = i == half - 1
        for p in range(PIECES):
            relay_two(i, p)
            if last and p == PIECES - 1:
                turned(i)

                @pl.when(sends_back)
                def _():
                    for j in range(i):
                        behind(i, c * half + j)
                        behind(i, (1 - c) * half + j)

            relay_one(i, p)
        if not last:
            turned(i)

        @pl.when(sends_back)
        def _():
            for h in range(i + 1):
                behind(h, mine)

        @pl.when(has_one)
        def _():
            received(s1, x1_sem, i)

        @pl.when(sends_back)
        def _():
            for h in range(i + 1):
                behind(h, theirs)

        @pl.when(has_one)
        def _():
            tile(1, s1, mine)
            tile(1, s1, theirs)

        @pl.when(has_up)
        def _():
            tile(2, s2, mine)
            received(s2, x2_sem, i)
            tile(2, s2, theirs)

    store(1).start()
    store(2).start()

    def back_store(h, ch):
        rows = pl.ds(h * width, width)
        cols = pl.ds(pl.multiple_of(ch * width, width), width)
        return pltpu.make_async_copy(
            r3r.at[h, ch], out_ref.at[WIN - 1, rows, cols], out3_sem.at[h, ch]
        )

    parts = []
    for i in range(half):
        for j in range(i):
            parts += [(i, 0, j), (i, 1, j)]
        for side in range(2):
            for h in range(i + 1):
                parts.append((h, side, i))

    @pl.when(gets_back)
    def _():
        for h, side, j in parts:
            ch = (c if side == 0 else 1 - c) * half + j
            back_copy(h, ch, above).wait_recv()
            back_store(h, ch).start()
        for h, side, j in parts:
            back_store(h, (c if side == 0 else 1 - c) * half + j).wait()

    for i in range(half):
        own_out(i).wait_send()
        second_out(i).wait_send()

    def drain(slot, carry):
        i = slot // PIECES
        p = lax.rem(slot, PIECES)
        ch = c * half + i
        rows = pl.ds(pl.multiple_of(slot * tpiece, tpiece), tpiece)

        @pl.when(has_down)
        def _():
            ref = part(s0, ch, p)
            remote(ref, ref, down_sem.at[slot], below).wait_send()

        @pl.when(jnp.logical_or(odd, has_up))
        def _():
            ref = part(s0, ch, p)
            remote(ref, ref, y_sem.at[slot], beside).wait_send()

        @pl.when(has_up)
        def _():
            remote(t0.at[rows, :], t0.at[rows, :], up_sem.at[slot], above).wait_send()
            ref = part(s2, ch, p)
            remote(ref, ref, x2_sem.at[slot], core).wait_send()

        @pl.when(has_one)
        def _():
            ref = part(s1, ch, p)
            remote(ref, ref, x1_sem.at[slot], core).wait_send()

        return carry

    lax.fori_loop(0, half * PIECES, drain, 0)

    @pl.when(sends_back)
    def _():
        for h in range(half):
            for ch in range(chunks):
                back_copy(h, ch, below).wait_send()

    for k in range(WIN - 1):
        store(k).wait()


def per_device(dosage, observed, counts):
    local, variants = dosage.shape
    n = lax.axis_size("var")
    full = local * lax.axis_size("samp")
    half = variants // 2
    width = 256
    chunks = variants // width
    slots = (chunks // 2) * PIECES
    dma = pltpu.SemaphoreType.DMA
    tiles = pl.pallas_call(
        functools.partial(kernel, n, float(full)),
        out_shape=jax.ShapeDtypeStruct((WIN, half, variants), jnp.bfloat16),
        in_specs=[pl.BlockSpec(memory_space=INPUT)] * 2,
        out_specs=pl.BlockSpec(memory_space=pl.ANY),
        scratch_shapes=[
            pltpu.VMEM((chunks, local, width), dosage.dtype),
            pltpu.VMEM((chunks, local, width), observed.dtype),
            pltpu.VMEM((chunks, full, width), jnp.bfloat16),
            pltpu.VMEM((chunks, full, width), jnp.bfloat16),
            pltpu.VMEM((chunks, full, width), jnp.bfloat16),
            pltpu.VMEM((half, full), jnp.bfloat16),
            pltpu.VMEM((half, full), jnp.bfloat16),
            pltpu.VMEM((chunks // 2, chunks, width, width), jnp.bfloat16),
            pltpu.VMEM((chunks // 2, chunks, width, width), jnp.bfloat16),
            pltpu.VMEM((chunks // 2, 8, 2 * width), jnp.float32),
            pltpu.VMEM((chunks // 2, 8, 2 * width), jnp.float32),
            pltpu.VMEM((WIN - 1, half, variants), jnp.bfloat16),
            dma((chunks, 2)),
            dma((chunks // 2, 2)),
            dma((chunks, 2)),
            dma((slots, 2)),
            dma((slots, 2)),
            dma((slots, 2)),
            dma((slots, 2)),
            dma((slots, 2)),
            dma((chunks // 2, chunks, 2)),
            dma((WIN - 1,)),
            dma((chunks // 2, chunks)),
        ],
        compiler_params=pltpu.CompilerParams(
            collective_id=0, has_side_effects=True, vmem_limit_bytes=VMEM_LIMIT
        ),
    )(pltpu.with_memory_space_constraint(dosage, pltpu.HBM), pltpu.with_memory_space_constraint(observed, pltpu.HBM))
    keep = jnp.arange(WIN, dtype=jnp.int32)[:, None, None] < counts[0]
    return jnp.where(keep, tiles, jnp.zeros_like(tiles))[None]


def solution(mesh):
    in_specs = (P("samp", ("region", "var")), P("samp", ("region", "var")), P(("region", "var")))
    out_specs = P(("region", "var"), None, "samp", None)
    return jax.shard_map(
        per_device, mesh=mesh, in_specs=in_specs, out_specs=out_specs, check_vma=False
    )
```
